512 devices in a mesh: req: 64 (over x, y, core), tp: 8 (over z).
Axes of the slice: x: 4, y: 8, z: 8, core: 2. Of those that a mesh axis runs over, the one named last changes fastest.
Arguments:
- patches: bfloat16 [114688, 1664], P('req', 'tp'), may hold values from -48 to 48
- ln_gain: bfloat16 [1664], P('tp'), may hold values from 0.099609375 to 1.8984375
- ln_bias: bfloat16 [1664], P('tp'), may hold values from -3 to 3
- merge_weight: bfloat16 [4, 1664, 1664], P(None, 'tp'), may hold values from -0.078125 to 0.078125
- text_rows: bfloat16 [32768, 1664], P('req', 'tp'), may hold values from -48 to 48
- norm_gain: bfloat16 [1664], replicated, may hold values from 0.099609375 to 1.8984375
- qkv_weight: bfloat16 [1664, 4992], P('req', 'tp'), may hold values from -0.15625 to 0.15625
- token_pos: int32 [28672], P('req'), may hold values from 0 to 32767, as said below
- text_len: int32 [8], replicated, may hold values from 1 to 4096, as said below
Outputs:
- qkv_rows: bfloat16 [32768, 4992], P('req', 'tp')
The draws below stay inside these ranges and needn't reach their ends.
Inputs may be any that keep to these rules, and one draw needn't show every extreme that they name: `token_pos`: all distinct. A device's merged tokens form 32 images of consecutive rows, each a multiple of 2 and at most 16 tokens, each written to consecutive positions that one device holds; a device's images go to 32 different devices and every device receives exactly 32 images. In every draw some image has 16 tokens. `text_len`: every image position of a request lies below its length.
All inputs are finite; a program needn't handle non-finite values.
Results may differ from the reference program's by a relative error of at most 0.0063.
Values may be sent and summed in bfloat16 or wider, within the bound.
A program may use at most 128 MiB of HBM per device.

```python
import math
import jax
import jax.numpy as jnp
from jax import lax

DV = 1664
D = 1664
TXT_DEV = 512
SEQ = 4096
IMG_CAP = 16
IMGS = 32
M_DEV = 448
PATCHES = 114688
MERGED = 28672
TOKENS = 32768
REQS = 8
QKV = 4992
N_REQ = 64


def image_layout(key):
    devices = N_REQ
    quantum = IMG_CAP // 8
    stride = devices // IMGS
    slot_total = IMGS * 7
    subkeys = jax.random.split(jax.random.fold_in(key, 7), 6)
    perm_keys = jax.random.split(subkeys[0], devices)
    ranks = jax.vmap(lambda one_key: jax.random.permutation(one_key, slot_total))(perm_keys).astype(jnp.int32)
    forced_dev = jax.random.randint(subkeys[1], (), 0, devices)
    forced_img = jax.random.randint(subkeys[2], (), 0, IMGS)
    slot_image = jnp.arange(slot_total, dtype=jnp.int32) // 7
    forced = (jnp.arange(devices, dtype=jnp.int32)[:, None] == forced_dev) & (slot_image[None, :] == forced_img)
    scores = jnp.where(forced, ranks - slot_total, ranks)
    order = jnp.argsort(scores, axis=1)
    placed = jnp.argsort(order, axis=1)
    chosen = (placed < 6 * IMGS).astype(jnp.int32)
    counts = jnp.sum(chosen.reshape(devices, IMGS, 7), axis=2)
    image_sizes = quantum * (1 + counts)
    image_ids = jnp.arange(IMGS, dtype=jnp.int32)
    recv_source = (jnp.arange(devices, dtype=jnp.int32)[:, None] - image_ids[None, :] * stride) % devices
    recv_sizes = image_sizes[recv_source, image_ids[None, :]]
    spare = TXT_DEV - jnp.sum(recv_sizes, axis=1)
    weights = jax.random.randint(subkeys[3], (devices, IMGS + 1), 1, 64)
    gap_sizes = spare[:, None] * weights // jnp.sum(weights, axis=1, keepdims=True)
    local_start = jnp.cumsum(recv_sizes, axis=1) - recv_sizes + jnp.cumsum(gap_sizes[:, :IMGS], axis=1)
    receiver = jax.random.permutation(subkeys[4], devices).astype(jnp.int32)
    global_start = receiver[:, None] * TXT_DEV + local_start
    send_target = (jnp.arange(devices, dtype=jnp.int32)[:, None] + image_ids[None, :] * stride) % devices
    send_start = global_start[send_target, image_ids[None, :]]
    bounds = jnp.cumsum(image_sizes, axis=1)
    tokens = jnp.arange(M_DEV, dtype=jnp.int32)
    image_of = jnp.sum((tokens[None, :, None] >= bounds[:, None, :]).astype(jnp.int32), axis=2)
    offset_before = jnp.take_along_axis(bounds - image_sizes, image_of, axis=1)
    first_pos = jnp.take_along_axis(send_start, image_of, axis=1)
    positions_src = first_pos + tokens[None, :] - offset_before
    sender = jax.random.permutation(subkeys[5], devices).astype(jnp.int32)
    positions = jnp.zeros((devices, M_DEV), jnp.int32).at[sender].set(positions_src)
    return positions.reshape(-1).astype(jnp.int32)


def draw_token_pos(key, part):
    return image_layout(key)


def draw_text_len(key, part):
    positions = image_layout(key)
    request = positions // SEQ
    last_image = jax.ops.segment_max(positions % SEQ + 1, request, num_segments=REQS)
    last_image = jnp.maximum(last_image, 1)
    drawn_len = jax.random.randint(jax.random.fold_in(key, 11), (REQS,), SEQ // 2, SEQ + 1)
    return jnp.maximum(last_image, drawn_len).astype(jnp.int32)


def rough_field(key, row_total, col_total):
    subkeys = jax.random.split(key, 4)
    noise = jax.random.normal(subkeys[0], (row_total, col_total), jnp.float32)
    rising = math.log(3.0)
    row_scale = jnp.exp(jax.random.uniform(subkeys[1], (row_total, 1), jnp.float32, 0.0, math.log(10.0)))
    col_scale = jnp.exp(rising * jnp.arange(col_total, dtype=jnp.float32) / (col_total - 1) + jax.random.uniform(subkeys[2], (1, col_total), jnp.float32, -0.7, 0.7))
    offset = 0.5 * jax.random.normal(subkeys[3], (row_total, 1), jnp.float32)
    field = row_scale * (noise * col_scale + offset) / 3.0
    return jnp.clip(field, -48.0, 48.0)


def draw_patches(key, part):
    return rough_field(jax.random.fold_in(key, 21), PATCHES, DV).astype(jnp.bfloat16)


def draw_text_rows(key, part):
    return rough_field(jax.random.fold_in(key, 23), TOKENS, D).astype(jnp.bfloat16)


def steps_of(stream_key, extent, pieces, low, top_value):
    loudness, own = 1.0, jax.random.fold_in(stream_key, 6)
    for axis_at, blocks in pieces:
        heights = jnp.exp(jax.random.uniform(jax.random.fold_in(own, axis_at), (blocks,), jnp.float32, low / len(pieces), top_value / len(pieces)))
        loudness = loudness * jnp.repeat(heights, extent[axis_at] // blocks).reshape([-1 if axis == axis_at else 1 for axis in range(len(extent))])
    return loudness


def bell_draw(rng, shape, width, reach, shards=(), held_as=jnp.bfloat16):
    array = width * jax.random.normal(rng, shape, jnp.float32)
    if shards:
        array = array * steps_of(rng, shape, shards, -0.22, 0.18)
    return jnp.clip(array, -reach, reach).astype(held_as)


def setup_inputs(seed: int = 0) -> dict:
    splits = jax.random.split(jax.random.key(seed), 10)
    patches = draw_patches(jax.random.fold_in(splits[9], 71), 0)
    ln_gain = jnp.clip(1.0 + 0.18 * jax.random.normal(splits[1], (DV,), jnp.float32), 0.099609375, 1.8984375).astype(jnp.bfloat16)
    ln_bias = bell_draw(splits[2], (DV,), 0.5, 3.0, ((0, 8),))
    merge_weight = bell_draw(splits[3], (4, DV, D), (4 * DV) ** -0.5, 0.078125, ((1, 8),))
    text_rows = draw_text_rows(jax.random.fold_in(splits[9], 71), 0)
    norm_gain = jnp.clip(1.0 + 0.18 * jax.random.normal(splits[5], (D,), jnp.float32), 0.099609375, 1.8984375).astype(jnp.bfloat16)
    qkv_weight = bell_draw(splits[6], (D, QKV), D ** -0.5, 0.15625, ((0, 64), (1, 8)))
    token_pos = draw_token_pos(jax.random.fold_in(splits[9], 71), 0)
    text_len = draw_text_len(jax.random.fold_in(splits[9], 71), 0)
    return {"patches": patches, "ln_gain": ln_gain, "ln_bias": ln_bias, "merge_weight": merge_weight, "text_rows": text_rows, "norm_gain": norm_gain, "qkv_weight": qkv_weight, "token_pos": token_pos, "text_len": text_len}


EPSILON = 1e-06

def reference(patches, ln_gain, ln_bias, merge_weight, text_rows, norm_gain, qkv_weight, token_pos, text_len):
    values = patches.astype(jnp.float32)
    row_mean = lax.optimization_barrier(jnp.sum(values, axis=1, keepdims=True)) / DV
    second = lax.optimization_barrier(jnp.sum(values * values, axis=1, keepdims=True)) / DV
    normed = ((values - row_mean) * lax.rsqrt(second - row_mean * row_mean + EPSILON) * ln_gain.astype(jnp.float32) + ln_bias.astype(jnp.float32)).astype(jnp.bfloat16)
    grouped = normed.reshape(MERGED, 4 * DV)
    merged = jnp.dot(grouped, merge_weight.reshape(4 * DV, D), preferred_element_type=jnp.float32).astype(jnp.bfloat16)
    combined = text_rows.at[token_pos].set(merged)
    full_rows = combined.astype(jnp.float32)
    scaled = (full_rows * lax.rsqrt(lax.optimization_barrier(jnp.mean(full_rows * full_rows, axis=1, keepdims=True)) + EPSILON) * norm_gain.astype(jnp.float32)).astype(jnp.bfloat16)
    projected = jnp.dot(scaled, qkv_weight, preferred_element_type=jnp.float32)
    position = jnp.arange(TOKENS, dtype=jnp.int32)
    limits = text_len[position // SEQ]
    keep_row = position % SEQ < limits
    return jnp.where(keep_row[:, None], projected, 0.0).astype(jnp.bfloat16)
```

```python
import functools

import jax
import jax.numpy as jnp
from jax import lax
from jax.experimental import pallas as pl
from jax.experimental.pallas import tpu as pltpu
from jax.sharding import PartitionSpec as P

EPSILON = 1e-06
SEQ = 4096
MESH = pl.DeviceIdType.MESH
SLOT = 16
F32 = jnp.float32
BF16 = jnp.bfloat16


def nt_dot(a, b):
    return lax.dot_general(a, b, (((1,), (1,)), ((), ())), preferred_element_type=F32)


def nn_dot(a, b):
    return lax.dot_general(a, b, (((1,), (0,)), ((), ())), preferred_element_type=F32)


def tn_dot(a, b):
    return lax.dot_general(a, b, (((0,), (0,)), ((), ())), preferred_element_type=F32)


def kernel(
    nx, ny, nc, nz,
    patches, ln_gain, ln_bias, merge_weight, text_rows, norm_gain, qkv_weight, token_pos, text_len,
    out,
    weight, values, stats, columns, partial_t, rs_send, rs_recv, merged, select, slots, landed, text_t,
    full, gathered, expanded, scaled_weight, total, gain_column, tokens,
    local_sem, stat_send, stat_recv, rs_send_sem, rs_recv_sem, slot_send, slot_recv,
    ag_send_sem, ag_recv_sem, wy_send, wy_recv, wx_send, wx_recv, wc_send, wc_recv,
):
    nr = nx * ny * nc
    rows, width = patches.shape
    windows = rows // 4
    text = text_rows.shape[0]
    model = nz * width
    depth = qkv_weight.shape[0]
    z = lax.axis_index("tp")
    c = lax.axis_index("req")
    core = lax.rem(c, nc)
    y = lax.rem(c // nc, ny)
    x = c // (nc * ny)

    def wrap(value):
        return lax.rem(value + nz, nz)

    def wait_bytes(ref, sem):
        pltpu.make_async_copy(ref, ref, sem).wait()

    fetch = pltpu.make_async_copy(merge_weight, weight, local_sem.at[0])
    fetch.start()

    barrier = pltpu.get_barrier_semaphore()

    @pl.loop(1, nz)
    def _(k):
        pl.semaphore_signal(barrier, inc=1, device_id=(c, lax.rem(z + k, nz)), device_id_type=MESH)

    @pl.loop(1, nr)
    def _(k):
        pl.semaphore_signal(barrier, inc=1, device_id=(lax.rem(c + k, nr), z), device_id_type=MESH)

    raw = patches[...]
    wide = raw.astype(F32)
    square = wide * wide
    high = square.astype(BF16)
    low = (square - high.astype(F32)).astype(BF16)
    ones = jnp.ones((8, width), BF16)
    sums = nt_dot(ones, raw)
    squares = nt_dot(ones, high) + nt_dot(ones, low)
    stats[z, 0:1, :] = sums[0:1, :]
    stats[z, 1:2, :] = squares[0:1, :]
    for p in range(values.shape[0]):
        size = min(128, width - p * 128)
        values[p, :, 0:size] = wide[:, p * 128 : p * 128 + size]

    pl.semaphore_wait(barrier, nz - 1 + nr - 1)

    @pl.loop(1, nz)
    def _(k):
        pltpu.make_async_remote_copy(
            stats.at[z], stats.at[z], stat_send, stat_recv,
            device_id=(c, lax.rem(z + k, nz)), device_id_type=MESH,
        ).start()

    own = pltpu.make_async_copy(qkv_weight, gathered.at[core, x, y], local_sem.at[1])
    own.start()

    @pl.loop(1, ny)
    def _(k):
        there = (x * ny + lax.rem(y + k, ny)) * nc + core
        pltpu.make_async_remote_copy(
            qkv_weight, gathered.at[core, x, y], wy_send, wy_recv,
            device_id=(there, z), device_id_type=MESH,
        ).start()

    tokens[...] = jnp.full(tokens.shape, -text, jnp.int32)
    tokens[0:1, 0:windows] = token_pos[...]
    place = tokens[...]
    receiver = place // text
    lane = lax.broadcasted_iota(jnp.int32, place.shape, 1)
    rank = jnp.zeros(place.shape, jnp.int32)
    for k in range(1, SLOT):
        before = pltpu.roll(receiver, k, 1)
        rank += jnp.where((before == receiver) & (lane >= k), 1, 0)
    slot = (receiver * SLOT + rank)[0:1, :]
    inner = lax.rem(place, text)[0:1, :]
    step_rows = select.shape[1]
    for q in range(select.shape[0]):
        wanted = lax.broadcasted_iota(jnp.int32, (step_rows, place.shape[1]), 0) + q * step_rows
        select[q] = jnp.where(wanted == slot, 1.0, 0.0).astype(BF16)
    merged[...] = jnp.zeros(merged.shape, BF16)
    info_rows = lax.broadcasted_iota(jnp.int32, (16, place.shape[1]), 0)
    info = jnp.where(
        info_rows == 0, lax.rem(inner, 16), jnp.where(info_rows == 1, inner // 16, jnp.where(info_rows == 2, 1, 0))
    )
    merged[width : width + 16, :] = info.astype(F32).astype(BF16)
    text_t[...] = text_rows[...].astype(F32).T
    gain_column[...] = jnp.broadcast_to(norm_gain[...].astype(F32), (8, model)).T

    wait_bytes(stats.at[pl.ds(0, nz - 1)], stat_recv)
    wait_bytes(stats.at[pl.ds(0, nz - 1)], stat_send)
    whole = stats[0]
    for k in range(1, nz):
        whole = whole + stats[k]
    whole = whole / model
    mean = whole[0:1, :]
    scale = lax.rsqrt(whole[1:2, :] - mean * mean + EPSILON)
    which = lax.broadcasted_iota(jnp.int32, (8, rows), 0)
    columns[:, 0:8] = jnp.where(which == 0, mean, scale).T
    gain = ln_gain[...].astype(F32)
    bias = ln_bias[...].astype(F32)
    parts = []
    for k in range(4):
        one = jnp.concatenate(
            [values[p, pl.ds(k, windows, stride=4), :] for p in range(values.shape[0])], axis=1
        )[:, 0:width]
        stat = columns[pl.ds(k, windows, stride=4), :]
        parts.append(((one - stat[:, 0:1]) * stat[:, 1:2] * gain + bias).astype(BF16))

    fetch.wait()
    start = 0
    while start < model:
        size = min(256, model - start)
        tile = None
        for k in range(4):
            term = nn_dot(parts[k], weight[k * width : (k + 1) * width, start : start + size])
            tile = term if tile is None else tile + term
        partial_t[start : start + size, :] = tile.T
        start += size

    half = (width // 2 + 15) // 16 * 16
    spans = ((0, half), (half, width - half))
    chains = []
    for d in (0, 1):
        for h in (0, 1):
            chains.append((d, h, nz // 2 if d == h else nz - 1 - nz // 2))

    def ring_copy(sem_pair, source, target, d):
        step = 1 if d == 0 else -1
        return pltpu.make_async_remote_copy(
            source, target, sem_pair[0], sem_pair[1], device_id=(c, wrap(z + step)), device_id_type=MESH
        )

    def rs_copy(d, h, t):
        size = spans[h][1]
        return ring_copy(
            (rs_send_sem.at[d, h, t], rs_recv_sem.at[d, h, t]),
            rs_send.at[d, h, t, pl.ds(0, size)],
            rs_recv.at[d, h, t, pl.ds(0, size)],
            d,
        )

    def rows_of(block, h):
        at, size = spans[h]
        return partial_t[pl.ds(pl.multiple_of(block * width + at, 8), size), :]

    steps = nz // 2
    for t in range(steps):
        for d, h, length in chains:
            if t >= length:
                continue
            size = spans[h][1]
            step = 1 if d == 0 else -1
            value = rows_of(wrap(z + step * (length - t)), h)
            if t > 0:
                rs_copy(d, h, t - 1).wait_recv()
                value = value + rs_recv[d, h, t - 1, 0:size, :].astype(F32)
            rs_send[d, h, t, 0:size, :] = value.astype(BF16)
            rs_copy(d, h, t).start()
        if t == 1:
            own.wait()
            wait_bytes(gathered.at[core, x, pl.ds(0, ny - 1)], wy_recv)
            wait_bytes(gathered.at[core, x, pl.ds(0, ny - 1)], wy_send)

            @pl.loop(1, nx)
            def _(k):
                there = (lax.rem(x + k, nx) * ny + y) * nc + core
                pltpu.make_async_remote_copy(
                    gathered.at[core, x], gathered.at[core, x], wx_send, wx_recv,
                    device_id=(there, z), device_id_type=MESH,
                ).start()

    for h in (0, 1):
        at, size = spans[h]
        value = rows_of(z, h)
        for d, hh, length in chains:
            if hh == h:
                rs_copy(d, h, length - 1).wait_recv()
                value = value + rs_recv[d, h, length - 1, 0:size, :].astype(F32)
        merged[at : at + size, 0:windows] = value.astype(BF16)
    for d, h, length in chains:
        for t in range(length):
            rs_copy(d, h, t).wait_send()

    per = step_rows // SLOT
    token_rows = merged[...]
    for q in range(select.shape[0]):
        block = nt_dot(select[q], token_rows).astype(BF16)
        slots[q * per : (q + 1) * per] = block.reshape(per, SLOT, block.shape[1])
    keep_own = pltpu.make_async_copy(slots.at[c], landed.at[c], local_sem.at[2])
    keep_own.start()

    @pl.loop(1, nr)
    def _(k):
        there = lax.rem(c + k, nr)
        pltpu.make_async_remote_copy(
            slots.at[there], landed.at[c], slot_send, slot_recv, device_id=(there, z), device_id_type=MESH
        ).start()

    wait_bytes(gathered.at[core, pl.ds(0, nx - 1)], wx_recv)
    wait_bytes(gathered.at[core, pl.ds(0, nx - 1)], wx_send)
    sibling = x * ny * nc + y * nc + (nc - 1 - core)
    swap = pltpu.make_async_remote_copy(
        gathered.at[core], gathered.at[core], wc_send, wc_recv, device_id=(sibling, z), device_id_type=MESH
    )
    swap.start()
    swap.wait()
    for ic in range(nc):
        for ix in range(nx):
            for iy in range(ny):
                row = ((ix * ny + iy) * nc + ic) * depth
                expanded[row : row + depth, :] = gathered[ic, ix, iy].astype(F32)
    for d in range(nz):
        at = d * width
        scaled_weight[d] = (expanded[at : at + width, :] * gain_column[at : at + width, 0:1]).astype(BF16)

    keep_own.wait()
    wait_bytes(landed.at[pl.ds(0, nr - 1)], slot_recv)
    wait_bytes(slots.at[pl.ds(0, nr - 1)], slot_send)
    arrived = landed[...].reshape(nr * SLOT, landed.shape[2])
    info = arrived[:, width : width + 8].astype(F32)
    position = info[:, 1:2] * 16.0 + info[:, 0:1] + (info[:, 2:3] - 1.0) * (4.0 * text)
    position = position.astype(jnp.int32)
    spread = jnp.where(
        position == lax.broadcasted_iota(jnp.int32, (nr * SLOT, text), 1), 1.0, 0.0
    ).astype(BF16)
    placed = tn_dot(arrived, spread)
    covered = placed[width + 2 : width + 3, :] > 0.5
    full[z] = jnp.where(covered, placed[0:width, :], text_t[...]).astype(BF16)

    def ag_copy(d, h, t):
        step = 1 if d == 0 else -1
        at, size = spans[h]
        block = full.at[wrap(z - step * t), pl.ds(at, size)]
        return ring_copy((ag_send_sem.at[d, h, t], ag_recv_sem.at[d, h, t]), block, block, d)

    for d, h, length in chains:
        ag_copy(d, h, 0).start()

    def project(block):
        piece = full[block]
        wide = piece.astype(F32)
        return tn_dot(piece, scaled_weight[block]), jnp.sum(wide * wide, axis=0, keepdims=True)

    product, norm = project(z)
    total[...] = product
    for t in range(steps):
        for d, h, length in chains:
            if t < length:
                ag_copy(d, h, t).wait_recv()
                if t + 1 < length:
                    ag_copy(d, h, t + 1).start()
        for block in (z + t + 1, z - t - 1) if t + 1 < nz - t - 1 else (z + t + 1,):
            product, part = project(wrap(lax.rem(block, nz)))
            total[...] += product
            norm = norm + part
    for d, h, length in chains:
        for t in range(length):
            ag_copy(d, h, t).wait_send()

    row_scale = lax.rsqrt(norm / model + EPSILON)
    row_scale = jnp.broadcast_to(row_scale, (8, text)).T[:, 0:1]
    per_request = SEQ // text
    limit = text_len[c // per_request]
    position = lax.broadcasted_iota(jnp.int32, (text, 1), 0) + lax.rem(c, per_request) * text
    out[...] = jnp.where(position < limit, total[...] * row_scale, 0.0).astype(BF16)


def solution(mesh, grid=None):
    nz = mesh.shape["tp"]
    nx, ny, nc = grid or (4, mesh.shape["req"] // 8, 2)

    def shards(
        patches, ln_gain, ln_bias, merge_weight, text_rows, norm_gain, qkv_weight, token_pos, text_len
    ):
        rows, width = patches.shape
        windows = rows // 4
        text = text_rows.shape[0]
        depth, heads = qkv_weight.shape
        model = nz * width
        nr = nx * ny * nc
        lanes = (windows + 127) // 128 * 128
        payload = (width + 16 + 127) // 128 * 128
        half = (width // 2 + 15) // 16 * 16
        steps = nz // 2
        chunk = min(256, nr * SLOT)
        dma = pltpu.SemaphoreType.DMA
        vmem = pl.BlockSpec(memory_space=pltpu.VMEM)
        return pl.pallas_call(
            functools.partial(kernel, nx, ny, nc, nz),
            out_shape=jax.ShapeDtypeStruct((text, heads), BF16),
            in_specs=[
                vmem, vmem, vmem, pl.BlockSpec(memory_space=pl.ANY), vmem, vmem, vmem, vmem,
                pl.BlockSpec(memory_space=pltpu.SMEM),
            ],
            out_specs=vmem,
            scratch_shapes=[
                pltpu.VMEM((4 * width, model), BF16),
                pltpu.VMEM(((width + 127) // 128, rows, 128), F32),
                pltpu.VMEM((nz, 2, rows), F32),
                pltpu.VMEM((rows, 128), F32),
                pltpu.VMEM((model, windows), F32),
                pltpu.VMEM((2, 2, steps, half, windows), BF16),
                pltpu.VMEM((2, 2, steps, half, windows), BF16),
                pltpu.VMEM((payload, lanes), BF16),
                pltpu.VMEM((nr * SLOT // chunk, chunk, lanes), BF16),
                pltpu.VMEM((nr, SLOT, payload), BF16),
                pltpu.VMEM((nr, SLOT, payload), BF16),
                pltpu.VMEM((width, text), F32),
                pltpu.VMEM((nz, width, text), BF16),
                pltpu.VMEM((nc, nx, ny, depth, heads), BF16),
                pltpu.VMEM((model, heads), F32),
                pltpu.VMEM((nz, width, heads), BF16),
                pltpu.VMEM((text, heads), F32),
                pltpu.VMEM((model, 8), F32),
                pltpu.VMEM((8, lanes), jnp.int32),
                dma((3,)), dma, dma, dma((2, 2, steps)), dma((2, 2, steps)), dma, dma,
                dma((2, 2, steps)), dma((2, 2, steps)), dma, dma, dma, dma, dma, dma,
            ],
            compiler_params=pltpu.CompilerParams(
                collective_id=0, has_side_effects=True, vmem_limit_bytes=56 << 20
            ),
        )(
            patches,
            ln_gain.reshape(1, width),
            ln_bias.reshape(1, width),
            merge_weight.reshape(4 * width, model),
            text_rows,
            norm_gain.reshape(1, model),
            qkv_weight,
            token_pos.reshape(1, windows),
            text_len,
        )

    placed = (
        P("req", "tp"),
        P("tp"),
        P("tp"),
        P(None, "tp", None),
        P("req", "tp"),
        P(),
        P("req", "tp"),
        P("req"),
        P(),
    )
    return jax.shard_map(
        shards, mesh=mesh, in_specs=placed, out_specs=P("req", "tp"), check_vma=False
    )
```

```python
import functools

import jax
import jax.numpy as jnp
from jax import lax
from jax.experimental import pallas as pl
from jax.experimental.pallas import tpu as pltpu
from jax.sharding import PartitionSpec as P

EPSILON = 1e-06
SEQ = 4096
MESH = pl.DeviceIdType.MESH
SLOT = 16
F32 = jnp.float32
BF16 = jnp.bfloat16


def nt_dot(a, b):
    return lax.dot_general(a, b, (((1,), (1,)), ((), ())), preferred_element_type=F32)


def nn_dot(a, b):
    return lax.dot_general(a, b, (((1,), (0,)), ((), ())), preferred_element_type=F32)


def tn_dot(a, b):
    return lax.dot_general(a, b, (((0,), (0,)), ((), ())), preferred_element_type=F32)


def halves(start, size):
    first = (size // 2 + 15) // 16 * 16
    return [(start, first), (start + first, size - first)]


def kernel(
    nx, ny, nc, nz,
    patches_hbm, gain_hbm, bias_hbm, merge_hbm, text_hbm, norm_hbm, qkv_hbm, token_pos, text_len,
    out_t,
    patches_t, ln_gain, ln_bias, weight, text_t, norm_gain,
    values, stats, columns, partial_t, rs_send, rs_recv, merged, select, slots, landed, spread,
    full, gathered, expanded, total, gain_column, tokens,
    local_sem, stat_send, stat_recv, rs_send_sem, rs_recv_sem, slot_send, slot_recv,
    ag_send_sem, ag_recv_sem, wy_send, wy_recv, wx_send, wx_recv, wc_send, wc_recv,
):
    nr = nx * ny * nc
    width, rows = patches_t.shape
    windows = rows // 4
    text = text_t.shape[1]
    model = nz * width
    depth = qkv_hbm.shape[0]
    z = lax.axis_index("tp")
    c = lax.axis_index("req")
    core = lax.rem(c, nc)
    y = lax.rem(c // nc, ny)
    x = c // (nc * ny)

    first_chunk = (width // 2 + 15) // 16 * 16
    chunks = ((0, first_chunk), (first_chunk, width - first_chunk))
    pieces = halves(*chunks[0]) + halves(*chunks[1])
    steps = nz // 2
    whole_tiles, rest = windows // 128, windows % 128
    assert rest == 64

    def reach(d, s):
        return steps if (d == 0) == (s in (0, 3)) else nz - 1 - steps

    def wrap(value):
        return lax.rem(value + nz, nz)

    def wait_bytes(ref, sem):
        pltpu.make_async_copy(ref, ref, sem).wait()

    barrier = pltpu.get_barrier_semaphore()

    @pl.loop(1, nz)
    def _(k):
        pl.semaphore_signal(barrier, inc=1, device_id=(c, lax.rem(z + k, nz)), device_id_type=MESH)

    fetches = [
        pltpu.make_async_copy(source, target, local_sem.at[i])
        for i, (source, target) in enumerate((
            (patches_hbm, patches_t), (gain_hbm, ln_gain), (bias_hbm, ln_bias), (merge_hbm, weight),
            (text_hbm, text_t), (norm_hbm, norm_gain), (qkv_hbm, gathered.at[core, x, y]),
        ))
    ]
    for fetch in fetches:
        fetch.start()

    @pl.loop(1, nr)
    def _(k):
        pl.semaphore_signal(barrier, inc=1, device_id=(lax.rem(c + k, nr), z), device_id_type=MESH)

    fetches[0].wait()
    wide = patches_t[...].astype(F32)
    stats[z, 0:1, :] = jnp.sum(wide, axis=0, keepdims=True)
    stats[z, 1:2, :] = jnp.sum(wide * wide, axis=0, keepdims=True)
    pl.semaphore_wait(barrier, nz - 1 + nr - 1)

    @pl.loop(1, nz)
    def _(k):
        pltpu.make_async_remote_copy(
            stats.at[z], stats.at[z], stat_send, stat_recv,
            device_id=(c, lax.rem(z + k, nz)), device_id_type=MESH,
        ).start()

    fetches[6].wait()

    @pl.loop(1, ny)
    def _(k):
        there = (x * ny + lax.rem(y + k, ny)) * nc + core
        pltpu.make_async_remote_copy(
            gathered.at[core, x, y], gathered.at[core, x, y], wy_send, wy_recv,
            device_id=(there, z), device_id_type=MESH,
        ).start()

    for p in range(values.shape[0]):
        size = min(128, width - p * 128)
        values[p, :, 0:size] = patches_t[p * 128 : p * 128 + size, :].astype(F32).T

    tokens[...] = jnp.full(tokens.shape, -text, jnp.int32)
    tokens[0:1, 0:windows] = token_pos[...]
    place = tokens[...]
    receiver = place // text
    lane = lax.broadcasted_iota(jnp.int32, place.shape, 1)
    rank = jnp.zeros(place.shape, jnp.int32)
    for k in range(1, SLOT):
        before = pltpu.roll(receiver, k, 1)
        rank += jnp.where((before == receiver) & (lane >= k), 1, 0)
    slot = (receiver * SLOT + rank)[0:1, :]
    inner = lax.rem(place, text)[0:1, :]
    step_rows = select.shape[1]
    for q in range(select.shape[0]):
        wanted = lax.broadcasted_iota(jnp.int32, (step_rows, place.shape[1]), 0) + q * step_rows
        select[q] = jnp.where(wanted == slot, 1.0, 0.0).astype(BF16)
    merged[...] = jnp.zeros(merged.shape, BF16)
    info_rows = lax.broadcasted_iota(jnp.int32, (16, place.shape[1]), 0)
    info = jnp.where(
        info_rows == 0, lax.rem(inner, 16), jnp.where(info_rows == 1, inner // 16, jnp.where(info_rows == 2, 1, 0))
    )
    merged[0, first_chunk : first_chunk + 16, :] = info.astype(F32).astype(BF16)
    fetches[1].wait()
    fetches[2].wait()
    fetches[4].wait()
    fetches[5].wait()
    gain_column[...] = jnp.broadcast_to(norm_gain[...].astype(F32).reshape(1, model), (8, model)).T
    gain = ln_gain[...].astype(F32).reshape(1, width)
    bias = ln_bias[...].astype(F32).reshape(1, width)
    fetches[3].wait()

    wait_bytes(stats.at[pl.ds(0, nz - 1)], stat_recv)
    wait_bytes(stats.at[pl.ds(0, nz - 1)], stat_send)
    whole = stats[0]
    for k in range(1, nz):
        whole = whole + stats[k]
    whole = whole / model
    mean = whole[0:1, :]
    scale = lax.rsqrt(whole[1:2, :] - mean * mean + EPSILON)
    which = lax.broadcasted_iota(jnp.int32, (8, rows), 0)
    columns[:, 0:8] = jnp.where(which == 0, mean, scale).T
    parts = []
    for k in range(4):
        one = jnp.concatenate(
            [values[p, pl.ds(k, windows, stride=4), :] for p in range(values.shape[0])], axis=1
        )[:, 0:width]
        stat = columns[pl.ds(k, windows, stride=4), :]
        parts.append(((one - stat[:, 0:1]) * stat[:, 1:2] * gain + bias).astype(BF16))

    start = 0
    while start < model:
        size = min(256, model - start)
        tile = None
        for k in range(4):
            term = nn_dot(parts[k], weight[k * width : (k + 1) * width, start : start + size])
            tile = term if tile is None else tile + term
        tile = tile.T
        for q in range(whole_tiles):
            partial_t[q, start : start + size, :] = tile[:, q * 128 : (q + 1) * 128]
        partial_t[whole_tiles, start : start + size, 0:rest] = tile[:, whole_tiles * 128 : windows]
        start += size

    wait_bytes(gathered.at[core, x, pl.ds(0, ny - 1)], wy_recv)
    wait_bytes(gathered.at[core, x, pl.ds(0, ny - 1)], wy_send)

    @pl.loop(1, nx)
    def _(k):
        there = (lax.rem(x + k, nx) * ny + y) * nc + core
        pltpu.make_async_remote_copy(
            gathered.at[core, x], gathered.at[core, x], wx_send, wx_recv,
            device_id=(there, z), device_id_type=MESH,
        ).start()

    def ring_copy(send, recv, source, target, d):
        step = 1 if d == 0 else -1
        return pltpu.make_async_remote_copy(
            source, target, send, recv, device_id=(c, wrap(z + step)), device_id_type=MESH
        )

    def packed_rows(s):
        size = pieces[s][1]
        return whole_tiles * size + size // 2

    def rs_copy(d, s, t):
        span = pl.ds(0, packed_rows(s))
        return ring_copy(
            rs_send_sem.at[d, s, t], rs_recv_sem.at[d, s, t],
            rs_send.at[d, s, t, span], rs_recv.at[d, s, t, span], d,
        )

    def own_rows(block, s):
        at, size = pieces[s]

        def load(tile, begin, count, lanes):
            return partial_t[tile, pl.ds(pl.multiple_of(block * width + begin, 8), count), 0:lanes]

        tiles = [load(q, at, size, 128) for q in range(whole_tiles)]
        low = load(whole_tiles, at, size // 2, rest)
        high = load(whole_tiles, at + size // 2, size // 2, rest)
        return jnp.concatenate(tiles + [jnp.concatenate([low, high], axis=1)], axis=0)

    order = [(s, d) for s in range(4) for d in (0, 1)]
    for t in range(steps):
        for s, d in order:
            if t >= reach(d, s):
                continue
            step = 1 if d == 0 else -1
            value = own_rows(wrap(z + step * (reach(d, s) - t)), s)
            if t > 0:
                rs_copy(d, s, t - 1).wait_recv()
                value = value + rs_recv[d, s, t - 1, 0 : packed_rows(s), :].astype(F32)
            rs_send[d, s, t, 0 : packed_rows(s), :] = value.astype(BF16)
            rs_copy(d, s, t).start()

    per = step_rows // SLOT

    def slot_copy(chunk, there):
        return pltpu.make_async_remote_copy(
            slots.at[chunk, there], landed.at[chunk, c], slot_send.at[chunk], slot_recv.at[chunk],
            device_id=(there, z), device_id_type=MESH,
        )

    for chunk in (0, 1):
        for s in (2 * chunk, 2 * chunk + 1):
            at, size = pieces[s]
            at -= chunks[chunk][0]
            value = own_rows(z, s)
            for d in (0, 1):
                rs_copy(d, s, reach(d, s) - 1).wait_recv()
                value = value + rs_recv[d, s, reach(d, s) - 1, 0 : packed_rows(s), :].astype(F32)
            for q in range(whole_tiles):
                merged[chunk, at : at + size, q * 128 : (q + 1) * 128] = value[q * size : (q + 1) * size].astype(BF16)
            for p in (0, 1):
                fold = value[whole_tiles * size :, p * rest : (p + 1) * rest]
                into = at + p * (size // 2)
                merged[chunk, into : into + size // 2, whole_tiles * 128 : windows] = fold.astype(BF16)
        token_rows = merged[chunk]
        for q in range(select.shape[0]):
            block = nt_dot(select[q], token_rows).astype(BF16)
            slots[chunk, q * per : (q + 1) * per] = block.reshape(per, SLOT, block.shape[1])
        keep_own = pltpu.make_async_copy(slots.at[chunk, c], landed.at[chunk, c], local_sem.at[7 + chunk])
        keep_own.start()

        @pl.loop(1, nr)
        def _(k):
            slot_copy(chunk, lax.rem(c + k, nr)).start()

    wait_bytes(gathered.at[core, pl.ds(0, nx - 1)], wx_recv)
    wait_bytes(gathered.at[core, pl.ds(0, nx - 1)], wx_send)
    sibling = x * ny * nc + y * nc + (nc - 1 - core)
    swap = pltpu.make_async_remote_copy(
        gathered.at[core], gathered.at[core], wc_send, wc_recv, device_id=(sibling, z), device_id_type=MESH
    )
    swap.start()
    for s, d in order:
        for t in range(reach(d, s)):
            rs_copy(d, s, t).wait_send()

    def ag_copy(d, s, t):
        step = 1 if d == 0 else -1
        at, size = pieces[s]
        block = full.at[wrap(z - step * t), pl.ds(at, size)]
        return ring_copy(ag_send_sem.at[d, s, t], ag_recv_sem.at[d, s, t], block, block, d)

    covered = None
    for chunk in (0, 1):
        at, size = chunks[chunk]
        pltpu.make_async_copy(slots.at[chunk, c], landed.at[chunk, c], local_sem.at[7 + chunk]).wait()
        wait_bytes(landed.at[chunk, pl.ds(0, nr - 1)], slot_recv.at[chunk])
        arrived = landed[chunk].reshape(nr * SLOT, landed.shape[3])
        if chunk == 0:
            info = arrived[:, size : size + 8].astype(F32)
            position = info[:, 1:2] * 16.0 + info[:, 0:1] + (info[:, 2:3] - 1.0) * (4.0 * text)
            position = position.astype(jnp.int32)
            spread[...] = jnp.where(
                position == lax.broadcasted_iota(jnp.int32, (nr * SLOT, text), 1), 1.0, 0.0
            ).astype(BF16)
        placed = tn_dot(arrived, spread[...])
        if chunk == 0:
            covered = placed[size + 2 : size + 3, :] > 0.5
        full[z, at : at + size, :] = jnp.where(
            covered, placed[0:size, :], text_t[at : at + size, :].astype(F32)
        ).astype(BF16)
        for s in (2 * chunk, 2 * chunk + 1):
            for d in (0, 1):
                ag_copy(d, s, 0).start()
    for chunk in (0, 1):
        wait_bytes(slots.at[chunk, pl.ds(0, nr - 1)], slot_send.at[chunk])
    swap.wait()

    group = width // depth

    def ready(block, i):
        for j in range(group):
            index = block * group + j
            expanded[i, j * depth : (j + 1) * depth, :] = gathered[
                lax.rem(index, nc), index // (nc * ny), lax.rem(index // nc, ny)
            ].astype(F32)
        gains = gain_column[pl.ds(pl.multiple_of(block * width, 8), width), :]
        return (expanded[i] * gains[:, 0:1]).astype(BF16)

    def project(block, block_weight):
        piece = full[block]
        wide = piece.astype(F32)
        return tn_dot(block_weight, piece), jnp.sum(wide * wide, axis=0, keepdims=True)

    product, norm = project(z, ready(z, 0))
    total[...] = product
    for t in range(steps):
        blocks = (z + t + 1, z - t - 1) if t + 1 < nz - t - 1 else (z + t + 1,)
        blocks = [wrap(lax.rem(block, nz)) for block in blocks]
        block_weights = [ready(block, i) for i, block in enumerate(blocks)]
        for s, d in order:
            if t < reach(d, s):
                ag_copy(d, s, t).wait_recv()
                if t + 1 < reach(d, s):
                    ag_copy(d, s, t + 1).start()
        for block, block_weight in zip(blocks, block_weights):
            product, part = project(block, block_weight)
            total[...] += product
            norm = norm + part

    row_scale = lax.rsqrt(norm / model + EPSILON)
    per_request = SEQ // text
    limit = text_len[c // per_request]
    position = lax.broadcasted_iota(jnp.int32, (1, text), 1) + lax.rem(c, per_request) * text
    out_t[...] = jnp.where(position < limit, total[...] * row_scale, 0.0).astype(BF16)
    for s, d in order:
        for t in range(reach(d, s)):
            ag_copy(d, s, t).wait_send()


def solution(mesh, grid=None):
    nz = mesh.shape["tp"]
    nx, ny, nc = grid or (4, mesh.shape["req"] // 8, 2)

    def shards(
        patches, ln_gain, ln_bias, merge_weight, text_rows, norm_gain, qkv_weight, token_pos, text_len
    ):
        rows, width = patches.shape
        windows = rows // 4
        text = text_rows.shape[0]
        depth, heads = qkv_weight.shape
        model = nz * width
        nr = nx * ny * nc
        lanes = (windows + 127) // 128 * 128
        first_chunk = (width // 2 + 15) // 16 * 16
        piece = halves(0, first_chunk)[0][1]
        packed = windows // 128 * piece + piece // 2
        steps = nz // 2
        chunk = min(256, nr * SLOT)
        dma = pltpu.SemaphoreType.DMA
        vmem = pl.BlockSpec(memory_space=pltpu.VMEM)
        hbm = pl.BlockSpec(memory_space=pl.ANY)
        ring = dma((2, 4, steps))
        return pl.pallas_call(
            functools.partial(kernel, nx, ny, nc, nz),
            out_shape=jax.ShapeDtypeStruct((heads, text), BF16),
            in_specs=[hbm] * 7 + [vmem, pl.BlockSpec(memory_space=pltpu.SMEM)],
            out_specs=vmem,
            scratch_shapes=[
                pltpu.VMEM((width, rows), BF16),
                pltpu.VMEM((width,), BF16),
                pltpu.VMEM((width,), BF16),
                pltpu.VMEM((4 * width, model), BF16),
                pltpu.VMEM((width, text), BF16),
                pltpu.VMEM((model,), BF16),
                pltpu.VMEM(((width + 127) // 128, rows, 128), F32),
                pltpu.VMEM((nz, 2, rows), F32),
                pltpu.VMEM((rows, 128), F32),
                pltpu.VMEM((windows // 128 + 1, model, 128), F32),
                pltpu.VMEM((2, 4, steps, packed, 128), BF16),
                pltpu.VMEM((2, 4, steps, packed, 128), BF16),
                pltpu.VMEM((2, 128, lanes), BF16),
                pltpu.VMEM((nr * SLOT // chunk, chunk, lanes), BF16),
                pltpu.VMEM((2, nr, SLOT, 128), BF16),
                pltpu.VMEM((2, nr, SLOT, 128), BF16),
                pltpu.VMEM((nr * SLOT, text), BF16),
                pltpu.VMEM((nz, width, text), BF16),
                pltpu.VMEM((nc, nx, ny, depth, heads), BF16),
                pltpu.VMEM((2, width, heads), F32),
                pltpu.VMEM((heads, text), F32),
                pltpu.VMEM((model, 8), F32),
                pltpu.VMEM((8, lanes), jnp.int32),
                dma((9,)), dma, dma, ring, ring, dma((2,)), dma((2,)), ring, ring,
                dma, dma, dma, dma, dma, dma,
            ],
            compiler_params=pltpu.CompilerParams(
                collective_id=0, has_side_effects=True, vmem_limit_bytes=56 << 20
            ),
        )(
            patches.T,
            ln_gain,
            ln_bias,
            merge_weight.reshape(4 * width, model),
            text_rows.T,
            norm_gain,
            qkv_weight,
            token_pos.reshape(1, windows),
            text_len,
        ).T

    placed = (
        P("req", "tp"),
        P("tp"),
        P("tp"),
        P(None, "tp", None),
        P("req", "tp"),
        P(),
        P("req", "tp"),
        P("req"),
        P(),
    )
    return jax.shard_map(
        shards, mesh=mesh, in_specs=placed, out_specs=P("req", "tp"), check_vma=False
    )
```

```python
import functools

import jax
import jax.numpy as jnp
from jax import lax
from jax.experimental import pallas as pl
from jax.experimental.pallas import tpu as pltpu
from jax.sharding import PartitionSpec as P

EPSILON = 1e-06
SEQ = 4096
MESH = pl.DeviceIdType.MESH
SLOT = 16
GROUPS = ((0,), (1,), (2,), (3,))
F32 = jnp.float32
BF16 = jnp.bfloat16


def nt_dot(a, b):
    return lax.dot_general(a, b, (((1,), (1,)), ((), ())), preferred_element_type=F32)


def nn_dot(a, b):
    return lax.dot_general(a, b, (((1,), (0,)), ((), ())), preferred_element_type=F32)


def tn_dot(a, b):
    return lax.dot_general(a, b, (((0,), (0,)), ((), ())), preferred_element_type=F32)


def halves(start, size):
    first = (size // 2 + 15) // 16 * 16
    return [(start, first), (start + first, size - first)]


def kernel(
    nx, ny, nc, nz,
    patches_hbm, gain_hbm, bias_hbm, merge_hbm, text_hbm, norm_hbm, qkv_hbm, token_pos, text_len,
    out_t,
    patches_t, ln_gain, ln_bias, weight, text_t, norm_gain,
    values, stats, columns, partial_t, rs_send, rs_recv, merged, select, slots, landed, spread,
    full, gathered, expanded, total, gain_column, tokens,
    local_sem, stat_send, stat_recv, rs_send_sem, rs_recv_sem, slot_send, slot_recv,
    ag_send_sem, ag_recv_sem, wy_send, wy_recv, wx_send, wx_recv, wc_send, wc_recv,
):
    nr = nx * ny * nc
    width, rows = patches_t.shape
    windows = rows // 4
    text = text_t.shape[1]
    model = nz * width
    depth = qkv_hbm.shape[0]
    z = lax.axis_index("tp")
    c = lax.axis_index("req")
    core = lax.rem(c, nc)
    y = lax.rem(c // nc, ny)
    x = c // (nc * ny)

    first_chunk = (width // 2 + 15) // 16 * 16
    chunks = ((0, first_chunk), (first_chunk, width - first_chunk))
    pieces = halves(*chunks[0]) + halves(*chunks[1])
    steps = nz // 2
    whole_tiles, rest = windows // 128, windows % 128
    assert rest == 64

    def reach(d, s):
        return steps if (d == 0) == (s in (0, 3)) else nz - 1 - steps

    def wrap(value):
        return lax.rem(value + nz, nz)

    def wait_bytes(ref, sem):
        pltpu.make_async_copy(ref, ref, sem).wait()

    barrier = pltpu.get_barrier_semaphore()

    @pl.loop(1, nz)
    def _(k):
        pl.semaphore_signal(barrier, inc=1, device_id=(c, lax.rem(z + k, nz)), device_id_type=MESH)

    fetches = [
        pltpu.make_async_copy(source, target, local_sem.at[i])
        for i, (source, target) in enumerate((
            (patches_hbm, patches_t), (gain_hbm, ln_gain), (bias_hbm, ln_bias), (merge_hbm, weight),
            (text_hbm, text_t), (norm_hbm, norm_gain), (qkv_hbm, gathered.at[core, x, y]),
        ))
    ]
    for fetch in fetches:
        fetch.start()

    @pl.loop(1, nr)
    def _(k):
        pl.semaphore_signal(barrier, inc=1, device_id=(lax.rem(c + k, nr), z), device_id_type=MESH)

    fetches[0].wait()
    wide = patches_t[...].astype(F32)
    stats[z, 0:1, :] = jnp.sum(wide, axis=0, keepdims=True)
    stats[z, 1:2, :] = jnp.sum(wide * wide, axis=0, keepdims=True)
    pl.semaphore_wait(barrier, nz - 1 + nr - 1)

    @pl.loop(1, nz)
    def _(k):
        pltpu.make_async_remote_copy(
            stats.at[z], stats.at[z], stat_send, stat_recv,
            device_id=(c, lax.rem(z + k, nz)), device_id_type=MESH,
        ).start()

    fetches[6].wait()

    @pl.loop(1, ny)
    def _(k):
        there = (x * ny + lax.rem(y + k, ny)) * nc + core
        pltpu.make_async_remote_copy(
            gathered.at[core, x, y], gathered.at[core, x, y], wy_send, wy_recv,
            device_id=(there, z), device_id_type=MESH,
        ).start()

    for p in range(values.shape[0]):
        size = min(128, width - p * 128)
        values[p, :, 0:size] = patches_t[p * 128 : p * 128 + size, :].astype(F32).T

    tokens[...] = jnp.full(tokens.shape, -text, jnp.int32)
    tokens[0:1, 0:windows] = token_pos[...]
    place = tokens[...]
    receiver = place // text
    lane = lax.broadcasted_iota(jnp.int32, place.shape, 1)
    rank = jnp.zeros(place.shape, jnp.int32)
    for k in range(1, SLOT):
        before = pltpu.roll(receiver, k, 1)
        rank += jnp.where((before == receiver) & (lane >= k), 1, 0)
    slot = (receiver * SLOT + rank)[0:1, :]
    inner = lax.rem(place, text)[0:1, :]
    step_rows = select.shape[1]
    for q in range(select.shape[0]):
        wanted = lax.broadcasted_iota(jnp.int32, (step_rows, place.shape[1]), 0) + q * step_rows
        select[q] = jnp.where(wanted == slot, 1.0, 0.0).astype(BF16)
    merged[...] = jnp.zeros(merged.shape, BF16)
    info_rows = lax.broadcasted_iota(jnp.int32, (16, place.shape[1]), 0)
    info = jnp.where(
        info_rows == 0, lax.rem(inner, 16), jnp.where(info_rows == 1, inner // 16, jnp.where(info_rows == 2, 1, 0))
    )
    merged[0, first_chunk : first_chunk + 16, :] = info.astype(F32).astype(BF16)
    fetches[1].wait()
    fetches[2].wait()
    fetches[4].wait()
    fetches[5].wait()
    gain_column[...] = jnp.broadcast_to(norm_gain[...].astype(F32).reshape(1, model), (8, model)).T
    gain = ln_gain[...].astype(F32).reshape(1, width)
    bias = ln_bias[...].astype(F32).reshape(1, width)
    fetches[3].wait()

    wait_bytes(stats.at[pl.ds(0, nz - 1)], stat_recv)
    wait_bytes(stats.at[pl.ds(0, nz - 1)], stat_send)
    whole = stats[0]
    for k in range(1, nz):
        whole = whole + stats[k]
    whole = whole / model
    mean = whole[0:1, :]
    scale = lax.rsqrt(whole[1:2, :] - mean * mean + EPSILON)
    which = lax.broadcasted_iota(jnp.int32, (8, rows), 0)
    columns[:, 0:8] = jnp.where(which == 0, mean, scale).T
    parts = []
    for k in range(4):
        one = jnp.concatenate(
            [values[p, pl.ds(k, windows, stride=4), :] for p in range(values.shape[0])], axis=1
        )[:, 0:width]
        stat = columns[pl.ds(k, windows, stride=4), :]
        parts.append(((one - stat[:, 0:1]) * stat[:, 1:2] * gain + bias).astype(BF16))

    def ring_copy(send, recv, source, target, d):
        step = 1 if d == 0 else -1
        return pltpu.make_async_remote_copy(
            source, target, send, recv, device_id=(c, wrap(z + step)), device_id_type=MESH
        )

    def piece_rows(s):
        return width if s < whole_tiles else width // 2

    def rs_copy(d, s, t):
        span = pl.ds(0, piece_rows(s))
        return ring_copy(
            rs_send_sem.at[d, s, t], rs_recv_sem.at[d, s, t],
            rs_send.at[d, s, t, span], rs_recv.at[d, s, t, span], d,
        )

    def own_rows(block, s):
        at = pl.multiple_of(block * width, 8)
        if s < whole_tiles:
            return partial_t[s, pl.ds(at, width), :]
        low = partial_t[s, pl.ds(at, width // 2), 0:rest]
        high = partial_t[s, pl.ds(at + width // 2, width // 2), 0:rest]
        return jnp.concatenate([low, high], axis=1)

    def rs_step(d, s, t):
        step = 1 if d == 0 else -1
        value = own_rows(wrap(z + step * (reach(d, s) - t)), s)
        if t > 0:
            rs_copy(d, s, t - 1).wait_recv()
            value = value + rs_recv[d, s, t - 1, 0 : piece_rows(s), :].astype(F32)
        rs_send[d, s, t, 0 : piece_rows(s), :] = value.astype(BF16)
        rs_copy(d, s, t).start()

    def x_stage():
        wait_bytes(gathered.at[core, x, pl.ds(0, ny - 1)], wy_recv)
        wait_bytes(gathered.at[core, x, pl.ds(0, ny - 1)], wy_send)

        @pl.loop(1, nx)
        def _(k):
            there = (lax.rem(x + k, nx) * ny + y) * nc + core
            pltpu.make_async_remote_copy(
                gathered.at[core, x], gathered.at[core, x], wx_send, wx_recv,
                device_id=(there, z), device_id_type=MESH,
            ).start()

    order = [(s, d) for s in range(4) for d in (0, 1)]
    for group in GROUPS:
        first, last = group[0] * 128, min((group[-1] + 1) * 128, windows)
        start = 0
        while start < model:
            size = min(256, model - start)
            tile = None
            for k in range(4):
                term = nn_dot(parts[k][first:last], weight[k * width : (k + 1) * width, start : start + size])
                tile = term if tile is None else tile + term
            tile = tile.T
            for s in group:
                at, lanes = s * 128 - first, min(128, windows - s * 128)
                partial_t[s, start : start + size, 0:lanes] = tile[:, at : at + lanes]
            start += size
        for s in group:
            for d in (0, 1):
                rs_step(d, s, 0)
    x_stage()
    for t in range(1, steps):
        for s, d in order:
            if t < reach(d, s):
                rs_step(d, s, t)

    per = step_rows // SLOT

    def slot_copy(chunk, there):
        return pltpu.make_async_remote_copy(
            slots.at[chunk, there], landed.at[chunk, c], slot_send.at[chunk], slot_recv.at[chunk],
            device_id=(there, z), device_id_type=MESH,
        )

    for s in range(4):
        value = own_rows(z, s)
        for d in (0, 1):
            rs_copy(d, s, reach(d, s) - 1).wait_recv()
            value = value + rs_recv[d, s, reach(d, s) - 1, 0 : piece_rows(s), :].astype(F32)
        value = value.astype(BF16)
        if s < whole_tiles:
            merged[0, 0:first_chunk, s * 128 : (s + 1) * 128] = value[0:first_chunk]
            merged[1, 0 : width - first_chunk, s * 128 : (s + 1) * 128] = value[first_chunk:]
        else:
            low, high, fold = value[:, 0:rest], value[:, rest : 2 * rest], width // 2
            merged[0, 0:fold, s * 128 : windows] = low
            merged[0, fold:first_chunk, s * 128 : windows] = high[0 : first_chunk - fold]
            merged[1, 0 : width - first_chunk, s * 128 : windows] = high[first_chunk - fold :]
    for chunk in (0, 1):
        token_rows = merged[chunk]
        for q in range(nx):
            there_x = lax.rem(x + q, nx)
            block = nt_dot(select[there_x], token_rows).astype(BF16)
            slots[chunk, pl.ds(there_x * per, per)] = block.reshape(per, SLOT, block.shape[1])
            if q == 0:
                pltpu.make_async_copy(slots.at[chunk, c], landed.at[chunk, c], local_sem.at[7 + chunk]).start()

            @pl.loop(1 if q == 0 else 0, per)
            def _(k):
                slot_copy(chunk, there_x * per + lax.rem(y * nc + core + k, per)).start()

    wait_bytes(gathered.at[core, pl.ds(0, nx - 1)], wx_recv)
    wait_bytes(gathered.at[core, pl.ds(0, nx - 1)], wx_send)
    sibling = x * ny * nc + y * nc + (nc - 1 - core)
    swap = pltpu.make_async_remote_copy(
        gathered.at[core], gathered.at[core], wc_send, wc_recv, device_id=(sibling, z), device_id_type=MESH
    )
    swap.start()
    for s, d in order:
        for t in range(reach(d, s)):
            rs_copy(d, s, t).wait_send()

    def ag_copy(d, s, t):
        step = 1 if d == 0 else -1
        at, size = pieces[s]
        block = full.at[wrap(z - step * t), pl.ds(at, size)]
        return ring_copy(ag_send_sem.at[d, s, t], ag_recv_sem.at[d, s, t], block, block, d)

    covered = None
    for chunk in (0, 1):
        at, size = chunks[chunk]
        pltpu.make_async_copy(slots.at[chunk, c], landed.at[chunk, c], local_sem.at[7 + chunk]).wait()
        wait_bytes(landed.at[chunk, pl.ds(0, nr - 1)], slot_recv.at[chunk])
        arrived = landed[chunk].reshape(nr * SLOT, landed.shape[3])
        if chunk == 0:
            info = arrived[:, size : size + 8].astype(F32)
            position = info[:, 1:2] * 16.0 + info[:, 0:1] + (info[:, 2:3] - 1.0) * (4.0 * text)
            position = position.astype(jnp.int32)
            spread[...] = jnp.where(
                position == lax.broadcasted_iota(jnp.int32, (nr * SLOT, text), 1), 1.0, 0.0
            ).astype(BF16)
        placed = tn_dot(arrived, spread[...])
        if chunk == 0:
            covered = placed[size + 2 : size + 3, :] > 0.5
        full[z, at : at + size, :] = jnp.where(
            covered, placed[0:size, :], text_t[at : at + size, :].astype(F32)
        ).astype(BF16)
        for s in (2 * chunk, 2 * chunk + 1):
            for d in (0, 1):
                ag_copy(d, s, 0).start()
    for chunk in (0, 1):
        wait_bytes(slots.at[chunk, pl.ds(0, nr - 1)], slot_send.at[chunk])
    swap.wait()

    group = width // depth

    def ready(block, i):
        for j in range(group):
            index = block * group + j
            expanded[i, j * depth : (j + 1) * depth, :] = gathered[
                lax.rem(index, nc), index // (nc * ny), lax.rem(index // nc, ny)
            ].astype(F32)
        gains = gain_column[pl.ds(pl.multiple_of(block * width, 8), width), :]
        return (expanded[i] * gains[:, 0:1]).astype(BF16)

    def project(block, block_weight):
        piece = full[block]
        wide = piece.astype(F32)
        return tn_dot(block_weight, piece), jnp.sum(wide * wide, axis=0, keepdims=True)

    product, norm = project(z, ready(z, 0))
    total[...] = product
    for t in range(steps):
        blocks = (z + t + 1, z - t - 1) if t + 1 < nz - t - 1 else (z + t + 1,)
        blocks = [wrap(lax.rem(block, nz)) for block in blocks]
        block_weights = [ready(block, i) for i, block in enumerate(blocks)]
        for s, d in order:
            if t < reach(d, s):
                ag_copy(d, s, t).wait_recv()
                if t + 1 < reach(d, s):
                    ag_copy(d, s, t + 1).start()
        for block, block_weight in zip(blocks, block_weights):
            product, part = project(block, block_weight)
            total[...] += product
            norm = norm + part

    row_scale = lax.rsqrt(norm / model + EPSILON)
    per_request = SEQ // text
    limit = text_len[c // per_request]
    position = lax.broadcasted_iota(jnp.int32, (1, text), 1) + lax.rem(c, per_request) * text
    out_t[...] = jnp.where(position < limit, total[...] * row_scale, 0.0).astype(BF16)
    for s, d in order:
        for t in range(reach(d, s)):
            ag_copy(d, s, t).wait_send()


def solution(mesh, grid=None):
    nz = mesh.shape["tp"]
    nx, ny, nc = grid or (4, mesh.shape["req"] // 8, 2)

    def shards(
        patches, ln_gain, ln_bias, merge_weight, text_rows, norm_gain, qkv_weight, token_pos, text_len
    ):
        rows, width = patches.shape
        windows = rows // 4
        text = text_rows.shape[0]
        depth, heads = qkv_weight.shape
        model = nz * width
        nr = nx * ny * nc
        lanes = (windows + 127) // 128 * 128
        first_chunk = (width // 2 + 15) // 16 * 16
        steps = nz // 2
        chunk = ny * nc * SLOT
        dma = pltpu.SemaphoreType.DMA
        vmem = pl.BlockSpec(memory_space=pltpu.VMEM)
        hbm = pl.BlockSpec(memory_space=pl.ANY)
        ring = dma((2, 4, steps))
        return pl.pallas_call(
            functools.partial(kernel, nx, ny, nc, nz),
            out_shape=pltpu.VMEM((heads, text), BF16),
            in_specs=[hbm] * 7 + [vmem, pl.BlockSpec(memory_space=pltpu.SMEM)],
            out_specs=vmem,
            scratch_shapes=[
                pltpu.VMEM((width, rows), BF16),
                pltpu.VMEM((width,), BF16),
                pltpu.VMEM((width,), BF16),
                pltpu.VMEM((4 * width, model), BF16),
                pltpu.VMEM((width, text), BF16),
                pltpu.VMEM((model,), BF16),
                pltpu.VMEM(((width + 127) // 128, rows, 128), F32),
                pltpu.VMEM((nz, 2, rows), F32),
                pltpu.VMEM((rows, 128), F32),
                pltpu.VMEM((windows // 128 + 1, model, 128), F32),
                pltpu.VMEM((2, 4, steps, width, 128), BF16),
                pltpu.VMEM((2, 4, steps, width, 128), BF16),
                pltpu.VMEM((2, 128, lanes), BF16),
                pltpu.VMEM((nx, chunk, lanes), BF16),
                pltpu.VMEM((2, nr, SLOT, 128), BF16),
                pltpu.VMEM((2, nr, SLOT, 128), BF16),
                pltpu.VMEM((nr * SLOT, text), BF16),
                pltpu.VMEM((nz, width, text), BF16),
                pltpu.VMEM((nc, nx, ny, depth, heads), BF16),
                pltpu.VMEM((2, width, heads), F32),
                pltpu.VMEM((heads, text), F32),
                pltpu.VMEM((model, 8), F32),
                pltpu.VMEM((8, lanes), jnp.int32),
                dma((9,)), dma, dma, ring, ring, dma((2,)), dma((2,)), ring, ring,
                dma, dma, dma, dma, dma, dma,
            ],
            compiler_params=pltpu.CompilerParams(
                collective_id=0, has_side_effects=True, vmem_limit_bytes=56 << 20
            ),
        )(
            patches.T,
            ln_gain,
            ln_bias,
            merge_weight.reshape(4 * width, model),
            text_rows.T,
            norm_gain,
            qkv_weight,
            token_pos.reshape(1, windows),
            text_len,
        ).T

    placed = (
        P("req", "tp"),
        P("tp"),
        P("tp"),
        P(None, "tp", None),
        P("req", "tp"),
        P(),
        P("req", "tp"),
        P("req"),
        P(),
    )
    return jax.shard_map(
        shards, mesh=mesh, in_specs=placed, out_specs=P("req", "tp"), check_vma=False
    )
```

```python
import functools

import jax
import jax.numpy as jnp
from jax import lax
from jax.experimental import pallas as pl
from jax.experimental.pallas import tpu as pltpu
from jax.sharding import PartitionSpec as P

EPSILON = 1e-06
SEQ = 4096
MESH = pl.DeviceIdType.MESH
SLOT = 16
GROUPS = ((0,), (1,), (2,), (3,))
F32 = jnp.float32
BF16 = jnp.bfloat16


def nt_dot(a, b):
    return lax.dot_general(a, b, (((1,), (1,)), ((), ())), preferred_element_type=F32)


def nn_dot(a, b):
    return lax.dot_general(a, b, (((1,), (0,)), ((), ())), preferred_element_type=F32)


def tn_dot(a, b):
    return lax.dot_general(a, b, (((0,), (0,)), ((), ())), preferred_element_type=F32)


def halves(start, size):
    first = (size // 2 + 15) // 16 * 16
    return [(start, first), (start + first, size - first)]


def kernel(
    nx, ny, nc, nz,
    patches_hbm, gain_hbm, bias_hbm, merge_hbm, text_hbm, norm_hbm, qkv_hbm, token_hbm, length_hbm,
    out_t,
    token_pos, text_len, patches_t, ln_gain, ln_bias, weight, text_t, norm_gain,
    values, stats, columns, partial_t, rs_send, rs_recv, merged, select, slots, landed, spread,
    full, gathered, expanded, total, gain_column, tokens,
    local_sem, stat_send, stat_recv, rs_send_sem, rs_recv_sem, slot_send, slot_recv,
    ag_send_sem, ag_recv_sem, wy_send, wy_recv, wx_send, wx_recv, wc_send, wc_recv,
):
    nr = nx * ny * nc
    width, rows = patches_t.shape
    windows = rows // 4
    text = text_t.shape[1]
    model = nz * width
    depth = qkv_hbm.shape[0]
    z = lax.axis_index("tp")
    c = lax.axis_index("req")
    core = lax.rem(c, nc)
    y = lax.rem(c // nc, ny)
    x = c // (nc * ny)

    first_chunk = (width // 2 + 15) // 16 * 16
    chunks = ((0, first_chunk), (first_chunk, width - first_chunk))
    pieces = halves(*chunks[0]) + halves(*chunks[1])
    steps = nz // 2
    whole_tiles, rest = windows // 128, windows % 128
    assert rest == 64

    def reach(d, s):
        return steps if (d == 0) == (s in (0, 3)) else nz - 1 - steps

    def wrap(value):
        return lax.rem(value + nz, nz)

    def wait_bytes(ref, sem):
        pltpu.make_async_copy(ref, ref, sem).wait()

    barrier = pltpu.get_barrier_semaphore()

    @pl.loop(1, nz)
    def _(k):
        pl.semaphore_signal(barrier, inc=1, device_id=(c, lax.rem(z + k, nz)), device_id_type=MESH)

    fetches = [
        pltpu.make_async_copy(source, target, local_sem.at[i])
        for i, (source, target) in enumerate((
            (patches_hbm, patches_t), (gain_hbm, ln_gain), (bias_hbm, ln_bias), (merge_hbm, weight),
            (text_hbm, text_t), (norm_hbm, norm_gain), (qkv_hbm, gathered.at[core, x, y]),
            (token_hbm, token_pos), (length_hbm, text_len),
        ))
    ]
    for fetch in fetches:
        fetch.start()

    @pl.loop(1, nr)
    def _(k):
        pl.semaphore_signal(barrier, inc=1, device_id=(lax.rem(c + k, nr), z), device_id_type=MESH)

    fetches[0].wait()
    wide = patches_t[...].astype(F32)
    stats[z, 0:1, :] = jnp.sum(wide, axis=0, keepdims=True)
    stats[z, 1:2, :] = jnp.sum(wide * wide, axis=0, keepdims=True)
    pl.semaphore_wait(barrier, nz - 1 + nr - 1)

    @pl.loop(1, nz)
    def _(k):
        pltpu.make_async_remote_copy(
            stats.at[z], stats.at[z], stat_send, stat_recv,
            device_id=(c, lax.rem(z + k, nz)), device_id_type=MESH,
        ).start()

    fetches[6].wait()

    @pl.loop(1, ny)
    def _(k):
        there = (x * ny + lax.rem(y + k, ny)) * nc + core
        pltpu.make_async_remote_copy(
            gathered.at[core, x, y], gathered.at[core, x, y], wy_send, wy_recv,
            device_id=(there, z), device_id_type=MESH,
        ).start()

    for p in range(values.shape[0]):
        size = min(128, width - p * 128)
        values[p, :, 0:size] = patches_t[p * 128 : p * 128 + size, :].astype(F32).T

    tokens[...] = jnp.full(tokens.shape, -text, jnp.int32)
    fetches[7].wait()
    tokens[0:1, 0:windows] = token_pos[...]
    place = tokens[...]
    receiver = place // text
    lane = lax.broadcasted_iota(jnp.int32, place.shape, 1)
    rank = jnp.zeros(place.shape, jnp.int32)
    for k in range(1, SLOT):
        before = pltpu.roll(receiver, k, 1)
        rank += jnp.where((before == receiver) & (lane >= k), 1, 0)
    slot = (receiver * SLOT + rank)[0:1, :]
    inner = lax.rem(place, text)[0:1, :]
    step_rows = select.shape[1]
    for q in range(select.shape[0]):
        wanted = lax.broadcasted_iota(jnp.int32, (step_rows, place.shape[1]), 0) + q * step_rows
        select[q] = jnp.where(wanted == slot, 1.0, 0.0).astype(BF16)
    merged[...] = jnp.zeros(merged.shape, BF16)
    info_rows = lax.broadcasted_iota(jnp.int32, (16, place.shape[1]), 0)
    info = jnp.where(
        info_rows == 0, lax.rem(inner, 16), jnp.where(info_rows == 1, inner // 16, jnp.where(info_rows == 2, 1, 0))
    )
    merged[0, first_chunk : first_chunk + 16, :] = info.astype(F32).astype(BF16)
    fetches[1].wait()
    fetches[2].wait()
    fetches[4].wait()
    fetches[5].wait()
    fetches[8].wait()
    gain_column[...] = jnp.broadcast_to(norm_gain[...].astype(F32).reshape(1, model), (8, model)).T
    gain = ln_gain[...].astype(F32).reshape(1, width)
    bias = ln_bias[...].astype(F32).reshape(1, width)
    fetches[3].wait()

    wait_bytes(stats.at[pl.ds(0, nz - 1)], stat_recv)
    wait_bytes(stats.at[pl.ds(0, nz - 1)], stat_send)
    whole = stats[0]
    for k in range(1, nz):
        whole = whole + stats[k]
    whole = whole / model
    mean = whole[0:1, :]
    scale = lax.rsqrt(whole[1:2, :] - mean * mean + EPSILON)
    which = lax.broadcasted_iota(jnp.int32, (8, rows), 0)
    columns[:, 0:8] = jnp.where(which == 0, mean, scale).T
    parts = []
    for k in range(4):
        one = jnp.concatenate(
            [values[p, pl.ds(k, windows, stride=4), :] for p in range(values.shape[0])], axis=1
        )[:, 0:width]
        stat = columns[pl.ds(k, windows, stride=4), :]
        parts.append(((one - stat[:, 0:1]) * stat[:, 1:2] * gain + bias).astype(BF16))

    def ring_copy(send, recv, source, target, d):
        step = 1 if d == 0 else -1
        return pltpu.make_async_remote_copy(
            source, target, send, recv, device_id=(c, wrap(z + step)), device_id_type=MESH
        )

    def piece_rows(s):
        return width if s < whole_tiles else width // 2

    def rs_copy(d, s, t):
        span = pl.ds(0, piece_rows(s))
        return ring_copy(
            rs_send_sem.at[d, s, t], rs_recv_sem.at[d, s, t],
            rs_send.at[d, s, t, span], rs_recv.at[d, s, t, span], d,
        )

    def own_rows(block, s):
        at = pl.multiple_of(block * width, 8)
        if s < whole_tiles:
            return partial_t[s, pl.ds(at, width), :]
        low = partial_t[s, pl.ds(at, width // 2), 0:rest]
        high = partial_t[s, pl.ds(at + width // 2, width // 2), 0:rest]
        return jnp.concatenate([low, high], axis=1)

    def rs_step(d, s, t):
        step = 1 if d == 0 else -1
        value = own_rows(wrap(z + step * (reach(d, s) - t)), s)
        if t > 0:
            rs_copy(d, s, t - 1).wait_recv()
            value = value + rs_recv[d, s, t - 1, 0 : piece_rows(s), :].astype(F32)
        rs_send[d, s, t, 0 : piece_rows(s), :] = value.astype(BF16)
        rs_copy(d, s, t).start()

    def x_stage():
        wait_bytes(gathered.at[core, x, pl.ds(0, ny - 1)], wy_recv)
        wait_bytes(gathered.at[core, x, pl.ds(0, ny - 1)], wy_send)

        @pl.loop(1, nx)
        def _(k):
            there = (lax.rem(x + k, nx) * ny + y) * nc + core
            pltpu.make_async_remote_copy(
                gathered.at[core, x], gathered.at[core, x], wx_send, wx_recv,
                device_id=(there, z), device_id_type=MESH,
            ).start()

    order = [(s, d) for s in range(4) for d in (0, 1)]
    for group in GROUPS:
        first, last = group[0] * 128, min((group[-1] + 1) * 128, windows)
        start = 0
        while start < model:
            size = min(256, model - start)
            tile = None
            for k in range(4):
                term = nn_dot(parts[k][first:last], weight[k * width : (k + 1) * width, start : start + size])
                tile = term if tile is None else tile + term
            tile = tile.T
            for s in group:
                at, lanes = s * 128 - first, min(128, windows - s * 128)
                partial_t[s, start : start + size, 0:lanes] = tile[:, at : at + lanes]
            start += size
        for s in group:
            for d in (0, 1):
                rs_step(d, s, 0)
    for t in range(1, steps):
        for s, d in order:
            if t < reach(d, s):
                rs_step(d, s, t)
        if t == 1:
            x_stage()

    per = step_rows // SLOT

    def slot_copy(chunk, there):
        return pltpu.make_async_remote_copy(
            slots.at[chunk, there], landed.at[chunk, c], slot_send.at[chunk], slot_recv.at[chunk],
            device_id=(there, z), device_id_type=MESH,
        )

    for s in range(4):
        value = own_rows(z, s)
        for d in (0, 1):
            rs_copy(d, s, reach(d, s) - 1).wait_recv()
            value = value + rs_recv[d, s, reach(d, s) - 1, 0 : piece_rows(s), :].astype(F32)
        value = value.astype(BF16)
        if s < whole_tiles:
            merged[0, 0:first_chunk, s * 128 : (s + 1) * 128] = value[0:first_chunk]
            merged[1, 0 : width - first_chunk, s * 128 : (s + 1) * 128] = value[first_chunk:]
        else:
            low, high, fold = value[:, 0:rest], value[:, rest : 2 * rest], width // 2
            merged[0, 0:fold, s * 128 : windows] = low
            merged[0, fold:first_chunk, s * 128 : windows] = high[0 : first_chunk - fold]
            merged[1, 0 : width - first_chunk, s * 128 : windows] = high[first_chunk - fold :]
    for chunk in (0, 1):
        token_rows = merged[chunk]
        for q in range(nx):
            there_x = lax.rem(x + q, nx)
            block = nt_dot(select[there_x], token_rows).astype(BF16)
            slots[chunk, pl.ds(there_x * per, per)] = block.reshape(per, SLOT, block.shape[1])
            if q == 0:
                pltpu.make_async_copy(slots.at[chunk, c], landed.at[chunk, c], local_sem.at[9 + chunk]).start()

            @pl.loop(1 if q == 0 else 0, per)
            def _(k):
                slot_copy(chunk, there_x * per + lax.rem(y * nc + core + k, per)).start()

    wait_bytes(gathered.at[core, pl.ds(0, nx - 1)], wx_recv)
    wait_bytes(gathered.at[core, pl.ds(0, nx - 1)], wx_send)
    sibling = x * ny * nc + y * nc + (nc - 1 - core)
    swap = pltpu.make_async_remote_copy(
        gathered.at[core], gathered.at[core], wc_send, wc_recv, device_id=(sibling, z), device_id_type=MESH
    )
    swap.start()
    for s, d in order:
        for t in range(reach(d, s)):
            rs_copy(d, s, t).wait_send()

    def ag_copy(d, s, t):
        step = 1 if d == 0 else -1
        at, size = pieces[s]
        block = full.at[wrap(z - step * t), pl.ds(at, size)]
        return ring_copy(ag_send_sem.at[d, s, t], ag_recv_sem.at[d, s, t], block, block, d)

    covered = None
    for chunk in (0, 1):
        at, size = chunks[chunk]
        pltpu.make_async_copy(slots.at[chunk, c], landed.at[chunk, c], local_sem.at[9 + chunk]).wait()
        wait_bytes(landed.at[chunk, pl.ds(0, nr - 1)], slot_recv.at[chunk])
        arrived = landed[chunk].reshape(nr * SLOT, landed.shape[3])
        if chunk == 0:
            info = arrived[:, size : size + 8].astype(F32)
            position = info[:, 1:2] * 16.0 + info[:, 0:1] + (info[:, 2:3] - 1.0) * (4.0 * text)
            position = position.astype(jnp.int32)
            spread[...] = jnp.where(
                position == lax.broadcasted_iota(jnp.int32, (nr * SLOT, text), 1), 1.0, 0.0
            ).astype(BF16)
        placed = tn_dot(arrived, spread[...])
        if chunk == 0:
            covered = placed[size + 2 : size + 3, :] > 0.5
        full[z, at : at + size, :] = jnp.where(
            covered, placed[0:size, :], text_t[at : at + size, :].astype(F32)
        ).astype(BF16)
        for s in (2 * chunk, 2 * chunk + 1):
            for d in (0, 1):
                ag_copy(d, s, 0).start()
    for chunk in (0, 1):
        wait_bytes(slots.at[chunk, pl.ds(0, nr - 1)], slot_send.at[chunk])
    swap.wait()

    group = width // depth

    def ready(block, i):
        for j in range(group):
            index = block * group + j
            expanded[i, j * depth : (j + 1) * depth, :] = gathered[
                lax.rem(index, nc), index // (nc * ny), lax.rem(index // nc, ny)
            ].astype(F32)
        gains = gain_column[pl.ds(pl.multiple_of(block * width, 8), width), :]
        return (expanded[i] * gains[:, 0:1]).astype(BF16)

    def project(block, block_weight):
        piece = full[block]
        wide = piece.astype(F32)
        return tn_dot(block_weight, piece), jnp.sum(wide * wide, axis=0, keepdims=True)

    def blocks_of(t):
        both = (z + t + 1, z - t - 1) if t + 1 < nz - t - 1 else (z + t + 1,)
        return [wrap(lax.rem(block, nz)) for block in both]

    for t in range(steps):
        for s, d in order:
            if t < reach(d, s):
                ag_copy(d, s, t).wait_recv()
                if t + 1 < reach(d, s):
                    ag_copy(d, s, t + 1).start()
        if t == 0:
            product, norm = project(z, ready(z, 2))
            total[...] = product
            block_weights = [ready(block, i) for i, block in enumerate(blocks_of(0))]
        for block, block_weight in zip(blocks_of(t), block_weights):
            product, part = project(block, block_weight)
            norm = norm + part
            if t + 1 < steps:
                total[...] += product
        if t + 1 < steps:
            block_weights = [ready(block, i) for i, block in enumerate(blocks_of(t + 1))]

    row_scale = lax.rsqrt(norm / model + EPSILON)
    per_request = SEQ // text
    limit = text_len[c // per_request]
    position = lax.broadcasted_iota(jnp.int32, (1, text), 1) + lax.rem(c, per_request) * text
    out_t[...] = jnp.where(position < limit, (total[...] + product) * row_scale, 0.0).astype(BF16)
    for s, d in order:
        for t in range(reach(d, s)):
            ag_copy(d, s, t).wait_send()


def solution(mesh, grid=None):
    nz = mesh.shape["tp"]
    nx, ny, nc = grid or (4, mesh.shape["req"] // 8, 2)

    def shards(
        patches, ln_gain, ln_bias, merge_weight, text_rows, norm_gain, qkv_weight, token_pos, text_len
    ):
        rows, width = patches.shape
        windows = rows // 4
        text = text_rows.shape[0]
        depth, heads = qkv_weight.shape
        model = nz * width
        nr = nx * ny * nc
        lanes = (windows + 127) // 128 * 128
        first_chunk = (width // 2 + 15) // 16 * 16
        steps = nz // 2
        chunk = ny * nc * SLOT
        dma = pltpu.SemaphoreType.DMA
        vmem = pl.BlockSpec(memory_space=pltpu.VMEM)
        hbm = pl.BlockSpec(memory_space=pl.ANY)
        ring = dma((2, 4, steps))
        return pl.pallas_call(
            functools.partial(kernel, nx, ny, nc, nz),
            out_shape=pltpu.VMEM((heads, text), BF16),
            in_specs=[hbm] * 9,
            out_specs=vmem,
            scratch_shapes=[
                pltpu.VMEM((1, windows), jnp.int32),
                pltpu.SMEM(text_len.shape, jnp.int32),
                pltpu.VMEM((width, rows), BF16),
                pltpu.VMEM((width,), BF16),
                pltpu.VMEM((width,), BF16),
                pltpu.VMEM((4 * width, model), BF16),
                pltpu.VMEM((width, text), BF16),
                pltpu.VMEM((model,), BF16),
                pltpu.VMEM(((width + 127) // 128, rows, 128), F32),
                pltpu.VMEM((nz, 2, rows), F32),
                pltpu.VMEM((rows, 128), F32),
                pltpu.VMEM((windows // 128 + 1, model, 128), F32),
                pltpu.VMEM((2, 4, steps, width, 128), BF16),
                pltpu.VMEM((2, 4, steps, width, 128), BF16),
                pltpu.VMEM((2, 128, lanes), BF16),
                pltpu.VMEM((nx, chunk, lanes), BF16),
                pltpu.VMEM((2, nr, SLOT, 128), BF16),
                pltpu.VMEM((2, nr, SLOT, 128), BF16),
                pltpu.VMEM((nr * SLOT, text), BF16),
                pltpu.VMEM((nz, width, text), BF16),
                pltpu.VMEM((nc, nx, ny, depth, heads), BF16),
                pltpu.VMEM((3, width, heads), F32),
                pltpu.VMEM((heads, text), F32),
                pltpu.VMEM((model, 8), F32),
                pltpu.VMEM((8, lanes), jnp.int32),
                dma((11,)), dma, dma, ring, ring, dma((2,)), dma((2,)), ring, ring,
                dma, dma, dma, dma, dma, dma,
            ],
            compiler_params=pltpu.CompilerParams(
                collective_id=0, has_side_effects=True, vmem_limit_bytes=56 << 20
            ),
        )(
            patches.T,
            ln_gain,
            ln_bias,
            merge_weight.reshape(4 * width, model),
            text_rows.T,
            norm_gain,
            qkv_weight,
            token_pos.reshape(1, windows),
            text_len,
        ).T

    placed = (
        P("req", "tp"),
        P("tp"),
        P("tp"),
        P(None, "tp", None),
        P("req", "tp"),
        P(),
        P("req", "tp"),
        P("req"),
        P(),
    )
    return jax.shard_map(
        shards, mesh=mesh, in_specs=placed, out_specs=P("req", "tp"), check_vma=False
    )
```
